128 devices in a mesh: box: 128 (over x, y, z, core).
Axes of the slice: x: 4, y: 4, z: 4, core: 2. Of those that a mesh axis runs over, the one named last changes fastest.
Arguments:
- sources: float32 [2048, 131072], P(None, 'box'), may hold values from -6 to 6
- leaf_basis: bfloat16 [256, 512, 256], P('box'), may hold values from -0.25 to 0.25
- stay_blocks: bfloat16 [8, 256, 256, 256], P(None, 'box'), may hold values from -0.25 to 0.25
- cross_blocks: bfloat16 [8, 256, 256, 256], P(None, 'box'), may hold values from -0.25 to 0.25
- out_basis: bfloat16 [256, 256, 512], P('box'), may hold values from -0.375 to 0.375
- near_blocks: bfloat16 [256, 768, 512], P('box'), may hold values from -0.21875 to 0.21875
Outputs:
- targets: float32 [2048, 131072], P(None, 'box')
The draws below stay inside these ranges and needn't reach their ends.
All inputs are finite; a program needn't handle non-finite values.
Results may differ from the reference program's by a relative error of at most 0.014.
Values may be sent and summed in bfloat16 or wider, within the bound.
A program may use at most 128 MiB of HBM per device.

```python
import jax
import jax.numpy as jnp

R = 256
B = 512
NV = 2048
H = 128
BOXES = 256
LEVELS = 8
POINTS = 131072


def steps_of(key, shape, split, least, top_value):
    loudness = 1.0
    for axis_at, blocks in split:
        heights = jax.random.uniform(jax.random.fold_in(jax.random.fold_in(key, 6), axis_at), (blocks,), jnp.float32, least / len(split), top_value / len(split))
        loudness = loudness * jnp.repeat(jnp.exp(heights), shape[axis_at] // blocks).reshape((-1,) + (1,) * (len(shape) - 1 - axis_at))
    return loudness


def normal_values(stream_key, extent, scale, most, split=(), kind=jnp.bfloat16):
    factor_of = steps_of(stream_key, extent, split, -0.22, 0.18) if split else 1.0
    drawn = jax.random.normal(stream_key, extent, jnp.float32) * scale * factor_of
    return jnp.minimum(jnp.maximum(drawn, -most), most).astype(kind)


def setup_inputs(seed: int = 0) -> dict:
    streams_of = jax.random.split(jax.random.key(seed), 7)
    sources = normal_values(streams_of[0], (NV, POINTS), 1.0, 6.0, ((1, 128),), jnp.float32)
    leaf_basis = normal_values(streams_of[1], (BOXES, B, R), B ** -0.5, 0.25, ((0, 128),))
    stay_blocks = normal_values(streams_of[2], (LEVELS, BOXES, R, R), (2 * R) ** -0.5, 0.25, ((1, 128),))
    cross_blocks = normal_values(streams_of[3], (LEVELS, BOXES, R, R), (2 * R) ** -0.5, 0.25, ((1, 128),))
    out_basis = normal_values(streams_of[4], (BOXES, R, B), R ** -0.5, 0.375, ((0, 128),))
    near_blocks = normal_values(streams_of[5], (BOXES, B + 2 * H, B), (B + 2 * H) ** -0.5, 0.21875, ((0, 128),))
    return dict(sources=sources, leaf_basis=leaf_basis, stay_blocks=stay_blocks, cross_blocks=cross_blocks, out_basis=out_basis, near_blocks=near_blocks)


def reference(sources, leaf_basis, stay_blocks, cross_blocks, out_basis, near_blocks):
    rounded = sources.astype(jnp.bfloat16)
    blocked = rounded.astype(jnp.float32).reshape(NV, BOXES, B)
    proxies = jnp.einsum("nbc,bcr->bnr", blocked, leaf_basis.astype(jnp.float32)).astype(jnp.bfloat16)
    for depth_at in range(LEVELS):
        wide = proxies.astype(jnp.float32)
        stay = jnp.einsum("bnr,brs->bns", wide, stay_blocks[depth_at].astype(jnp.float32))
        moved = jnp.einsum("bnr,brs->bns", wide, cross_blocks[depth_at].astype(jnp.float32))
        stride = 2 ** depth_at
        moved = moved.reshape(BOXES // (2 * stride), 2, stride, NV, R)[:, ::-1].reshape(BOXES, NV, R)
        proxies = (stay + moved).astype(jnp.bfloat16)
    far_field = jnp.einsum("bnr,brc->nbc", proxies.astype(jnp.float32), out_basis.astype(jnp.float32))
    padded = jnp.pad(rounded, ((0, 0), (H, H)))
    middle = padded[:, H:H + POINTS].reshape(NV, BOXES, B)
    left_rim = padded[:, :POINTS].reshape(NV, BOXES, B)[:, :, :H]
    right_rim = padded[:, 2 * H:2 * H + POINTS].reshape(NV, BOXES, B)[:, :, B - H:]
    window = jnp.concatenate([left_rim, middle, right_rim], axis=2).astype(jnp.float32)
    near_field = jnp.einsum("nbw,bwc->nbc", window, near_blocks.astype(jnp.float32))
    return (far_field + near_field).reshape(NV, POINTS)
```

```python
import jax
import jax.numpy as jnp
from jax import lax
from jax.experimental import pallas as pl
from jax.experimental.pallas import tpu as pltpu
from jax.sharding import PartitionSpec as P

MESH = pl.DeviceIdType.MESH
BF = jnp.bfloat16
F32 = jnp.float32

B = 512
H = 128
R = 256
NV = 2048
CH = 256
NC = NV // CH
NU = 2 * NC
HALF = CH // 2
SLOTS = 4

T_ONE = 1
T_IN = (3, 9, 15)
T_MID = (5, 11, 17)
T_BACK = (7, 13, 19)
T_HALO = 16
STEPS = NU + T_BACK[2]
STRIDE = (2, 8, 32)


def mm(a, b):
    return jnp.dot(a, b, preferred_element_type=F32)


def kernel(
    src_h, leaf_h, stay_h, cross_h, outb_h, near_h, out_h,
    src_v, leaf_v, stay_v, cross_v, outb_v, near_v,
    pstay, pcross, win, xs1, xr1, pn, rsw, ab, xs, xr, bs, obuf,
    l_src, l_w, l_out,
    r_one, r_in, r_mid, r_back, r_halo, r_w,
    s_one, s_in, s_mid, s_back, s_halo, s_w,
):
    me = lax.axis_index("box")
    core = me % 2
    mate = me + 1 - 2 * core
    pos = [(me // st) % 4 for st in STRIDE]
    a_of = [me + (1 - 2 * (v % 2)) * st for v, st in zip(pos, STRIDE)]
    b_of = [me + (3 - 2 * v) * st for v, st in zip(pos, STRIDE)]
    half = [(v % 2 + v // 2) % 2 for v in pos]
    count = lax.axis_size("box")
    right = (me + 1) % count
    left = (me + count - 1) % count

    def local(src, dst, sem):
        return pltpu.make_async_copy(src, dst, sem)

    def remote(src, dst, ssem, rsem, to):
        return pltpu.make_async_remote_copy(
            src_ref=src, dst_ref=dst, send_sem=ssem, recv_sem=rsem,
            device_id=(to,), device_id_type=MESH,
        )

    def src_copy(c):
        return local(src_h.at[pl.ds(c * CH, CH)], src_v.at[c % SLOTS], l_src.at[c])

    loads = [
        local(h, v, l_w.at[i])
        for i, (h, v) in enumerate(
            ((leaf_h, leaf_v), (stay_h, stay_v), (cross_h, cross_v), (near_h, near_v), (outb_h, outb_v))
        )
    ]
    src_copy(0).start()
    loads[0].start()
    loads[1].start()
    loads[2].start()

    barrier = pltpu.get_barrier_semaphore()
    peers = [mate] + a_of + b_of + [left, right]
    for to in peers:
        pl.semaphore_signal(barrier, inc=1, device_id=(to,), device_id_type=MESH)
    pl.semaphore_wait(barrier, len(peers))

    def w_copy(d, which):
        level = 2 + 2 * d + which // 2
        held, there = ((stay_h, pstay), (cross_h, pcross))[which % 2]
        return remote(held.at[level], there.at[d, which // 2], s_w.at[d, which], r_w.at[d, which], a_of[d])

    for which in (0, 1, 3):
        w_copy(0, which).start()
    for d in (1, 2):
        for which in range(4):
            w_copy(d, which).start()
    for c in range(1, SLOTS):
        src_copy(c).start()
    loads[3].start()
    loads[4].start()

    @pl.when(me == 0)
    def _():
        for c in range(NC):
            win[c, :, 0:H] = jnp.zeros((CH, H), BF)

    @pl.when(me == count - 1)
    def _():
        for c in range(NC):
            win[c, :, H + 2 * B :] = jnp.zeros((CH, H), BF)

    for i in range(3):
        loads[i].wait()

    def one_copy(u):
        return remote(xs1.at[u], xr1.at[u], s_one, r_one.at[u], mate)

    def in_copy(d, u):
        return remote(pn.at[d, u, 1 - half[d]], rsw.at[d, u], s_in.at[d], r_in.at[d, u], a_of[d])

    def mid_copy(d, u):
        return remote(xs.at[d, u], xr.at[d, u], s_mid.at[d], r_mid.at[d, u], b_of[d])

    def back_copy(d, u, mine):
        at = half[d] if mine else 1 - half[d]
        return remote(bs.at[d, u], pn.at[d + 1, u, at], s_back.at[d], r_back.at[d, u], a_of[d])

    def halo_copy(side, c):
        if side == 0:
            return remote(
                win.at[c, :, pl.ds(2 * B, H)], win.at[c, :, pl.ds(0, H)], s_halo.at[0], r_halo.at[0, c], right
            )
        return remote(
            win.at[c, :, pl.ds(H, H)], win.at[c, :, pl.ds(H + 2 * B, H)], s_halo.at[1], r_halo.at[1, c], left
        )

    def out_copy(u):
        return local(
            obuf.at[u],
            out_h.at[pl.ds((u // 2) * CH, CH), pl.ds(pl.multiple_of((u % 2) * B, B), B)],
            l_out,
        )

    def leaf_stage(c):
        src_copy(c).wait()
        for h in range(2):
            rows = pl.ds(h * HALF, HALF)
            cells = src_v[c % SLOTS, rows, :].astype(BF)
            win[c, rows, H : H + 2 * B] = cells
            p0 = mm(cells[:, :B], leaf_v[0]).astype(BF)
            p1 = mm(cells[:, B:], leaf_v[1]).astype(BF)
            n0 = (mm(p0, stay_v[0, 0]) + mm(p1, cross_v[0, 1])).astype(BF)
            n1 = (mm(p1, stay_v[0, 1]) + mm(p0, cross_v[0, 0])).astype(BF)
            pn[0, 2 * c, h] = n0
            pn[0, 2 * c + 1, h] = n1
            xs1[2 * c, h] = mm(n0, cross_v[1, 0]).astype(BF)
            xs1[2 * c + 1, h] = mm(n1, cross_v[1, 1]).astype(BF)
        one_copy(2 * c).start()
        one_copy(2 * c + 1).start()

        @pl.when(c + SLOTS < NC)
        def _():
            src_copy(c + SLOTS).start()

    def one_stage(u):
        b = u % 2
        one_copy(u).wait_recv()
        for h in range(2):
            pn[0, u, h] = (mm(pn[0, u, h], stay_v[1, b]) + xr1[u, h].astype(F32)).astype(BF)
        in_copy(0, u).start()

        @pl.when(u == 0)
        def _():
            w_copy(0, 2).start()

    def in_stage(d, u):
        b = u % 2
        lev = 2 + 2 * d

        @pl.when(u == 0)
        def _():
            for which in (0, 1, 3):
                w_copy(d, which).wait_recv()

        in_copy(d, u).wait_recv()
        pa = pn[d, u, half[d]]
        pb = rsw[d, u]
        na = (mm(pa, stay_v[lev, b]) + mm(pb, pcross[d, 0, b])).astype(BF)
        nb = (mm(pb, pstay[d, 0, b]) + mm(pa, cross_v[lev, b])).astype(BF)
        xs[d, u, 0] = mm(na, cross_v[lev + 1, b]).astype(BF)
        xs[d, u, 1] = mm(nb, pcross[d, 1, b]).astype(BF)
        ab[d, u % 4, 0] = na
        ab[d, u % 4, 1] = nb
        mid_copy(d, u).start()

    def mid_stage(d, u):
        b = u % 2
        lev = 3 + 2 * d

        @pl.when(u == 0)
        def _():
            w_copy(d, 2).wait_recv()

        mid_copy(d, u).wait_recv()
        bs[d, u] = (mm(ab[d, u % 4, 1], pstay[d, 1, b]) + xr[d, u, 0].astype(F32)).astype(BF)
        back_copy(d, u, True).start()
        pn[d + 1, u, half[d]] = (mm(ab[d, u % 4, 0], stay_v[lev, b]) + xr[d, u, 1].astype(F32)).astype(BF)

    def back_stage(d, u):
        back_copy(d, u, False).wait_recv()
        if d < 2:
            in_copy(d + 1, u).start()

    def out_stage(u):
        b = u % 2
        c = u // 2

        @pl.when(u == 0)
        def _():
            loads[3].wait()
            loads[4].wait()

        @pl.when((b == 0) & (me > 0))
        def _():
            halo_copy(0, c).wait_recv()

        @pl.when((b == 1) & (me < count - 1))
        def _():
            halo_copy(1, c).wait_recv()

        cols = pl.ds(pl.multiple_of(b * B, B), B + 2 * H)
        for h in range(2):
            rows = pl.ds(h * HALF, HALF)
            total = mm(win[c, rows, cols], near_v[b]) + mm(pn[3, u, h], outb_v[b])
            obuf[u, rows, :] = total.astype(BF)
        out_copy(u).start()

    def step(t, _):
        def stage(at, body, count_of=NU):
            u = t - at

            @pl.when((u >= 0) & (u < count_of))
            def _():
                body(u)

        def finish(u):
            back_stage(2, u)
            out_stage(u)

        stage(T_BACK[2], finish)
        for d in (2, 1, 0):
            if d < 2:
                stage(T_BACK[d], lambda u, d=d: back_stage(d, u))
            stage(T_MID[d], lambda u, d=d: mid_stage(d, u))
            stage(T_IN[d], lambda u, d=d: in_stage(d, u))
        stage(T_ONE, one_stage)

        @pl.when((t % 2 == 0) & (t < NU))
        def _():
            leaf_stage(t // 2)

        def halos(c):
            @pl.when(me < count - 1)
            def _():
                halo_copy(0, c).start()

            @pl.when(me > 0)
            def _():
                halo_copy(1, c).start()

        stage(T_HALO, halos, NC)
        return 0

    lax.fori_loop(0, STEPS, step, 0)

    local(obuf, obuf, l_out).wait()
    remote(xs1, xr1, s_one, r_one.at[0], mate).wait_send()
    for d in range(3):
        remote(rsw.at[d], rsw.at[d], s_in.at[d], r_in.at[d, 0], a_of[d]).wait_send()
        remote(xs.at[d], xr.at[d], s_mid.at[d], r_mid.at[d, 0], b_of[d]).wait_send()
        remote(bs.at[d], bs.at[d], s_back.at[d], r_back.at[d, 0], a_of[d]).wait_send()
        for which in range(4):
            w_copy(d, which).wait_send()
    whole = rsw.at[0, pl.ds(0, NC)]

    @pl.when(me < count - 1)
    def _():
        remote(whole, whole, s_halo.at[0], r_halo.at[0, 0], right).wait_send()

    @pl.when(me > 0)
    def _():
        remote(whole, whole, s_halo.at[1], r_halo.at[1, 0], left).wait_send()


def per_device(sources, leaf_basis, stay_blocks, cross_blocks, out_basis, near_blocks):
    dma = pltpu.SemaphoreType.DMA
    v = pltpu.VMEM
    scratch = [
        v((SLOTS, CH, 2 * B), F32),
        v(leaf_basis.shape, BF),
        v(stay_blocks.shape, BF),
        v(cross_blocks.shape, BF),
        v(out_basis.shape, BF),
        v(near_blocks.shape, BF),
        v((3, 2, 2, R, R), BF),
        v((3, 2, 2, R, R), BF),
        v((NC, CH, 2 * B + 2 * H), BF),
        v((NU, 2, HALF, R), BF),
        v((NU, 2, HALF, R), BF),
        v((4, NU, 2, HALF, R), BF),
        v((3, NU, HALF, R), BF),
        v((3, 4, 2, HALF, R), BF),
        v((3, NU, 2, HALF, R), BF),
        v((3, NU, 2, HALF, R), BF),
        v((3, NU, HALF, R), BF),
        v((NU, CH, B), BF),
        dma((NC,)), dma((5,)), dma,
        dma((NU,)), dma((3, NU)), dma((3, NU)), dma((3, NU)), dma((2, NC)), dma((3, 4)),
        dma, dma((3,)), dma((3,)), dma((3,)), dma((2,)), dma((3, 4)),
    ]
    out = pl.pallas_call(
        kernel,
        out_shape=jax.ShapeDtypeStruct((NV, 2 * B), BF),
        in_specs=[pl.BlockSpec(memory_space=pl.ANY)] * 6,
        out_specs=pl.BlockSpec(memory_space=pl.ANY),
        scratch_shapes=scratch,
        compiler_params=pltpu.CompilerParams(
            collective_id=0, has_side_effects=True, vmem_limit_bytes=66_900_000
        ),
    )(sources, leaf_basis, stay_blocks, cross_blocks, out_basis, near_blocks)
    return out.astype(F32)


def solution(mesh):
    in_specs = (
        P(None, "box"),
        P("box", None, None),
        P(None, "box", None, None),
        P(None, "box", None, None),
        P("box", None, None),
        P("box", None, None),
    )
    return jax.shard_map(
        per_device, mesh=mesh, in_specs=in_specs, out_specs=P(None, "box"), check_vma=False
    )
```

```python
import jax
import jax.numpy as jnp
from jax import lax
from jax.experimental import pallas as pl
from jax.experimental.pallas import tpu as pltpu
from jax.sharding import PartitionSpec as P

MESH = pl.DeviceIdType.MESH
BF = jnp.bfloat16
F32 = jnp.float32

B = 512
H = 128
R = 256
NV = 2048
CH = 256
NC = NV // CH
NU = 2 * NC
HALF = CH // 2
SLOTS = 4

STRIDE = (2, 8, 32)
AHEAD = 2
STAGES = (("in", 0), ("mid", 0), ("back", 0), ("in", 1), ("mid", 1), ("back", 1), ("in", 2), ("mid", 2), ("back", 2))
FIRST = 8
AT_A = (0, 2, 4, 5, 7, 9, 10, 12, 14)
AT_B = (0, 2, 4, 5, 7, 9, 10, 12, 14)
LAG_A = dict(zip(("in", "mid", "back"), (AT_A[0::3], AT_A[1::3], AT_A[2::3])))
LAG_B = dict(zip(("in", "mid", "back"), (AT_B[0::3], AT_B[1::3], AT_B[2::3])))
STEPS = NU + LAG_B["back"][2]
HALO_AT = NU + 1
OUT_AT = HALO_AT + 2
OUT_RATE = 3
PIECE_AT = (0, 1, 2, 3, 4, 5, 6, 6)
KEYS = 8
WROWS = 128


def mm(a, b):
    return jnp.dot(a, b, preferred_element_type=F32)


def kernel(
    src_h, leaf_h, stay_h, cross_h, outb_h, near_h, out_h,
    src_v, leaf_v, w0, wl, w1, w2, wo, win, xs1, xr1, st1, pn, rsw, st, xs, xr, bs, obuf,
    l_src, l_w, l_out,
    r_one, r_in, r_mid, r_back, r_halo, r_w,
    s_one, s_in, s_mid, s_back, s_halo, s_w,
):
    me = lax.axis_index("box")
    core = me % 2
    mate = me + 1 - 2 * core
    pos = [(me // st) % 4 for st in STRIDE]
    a_of = [me + (1 - 2 * (v % 2)) * st for v, st in zip(pos, STRIDE)]
    b_of = [me + (3 - 2 * v) * st for v, st in zip(pos, STRIDE)]
    half = [(v % 2 + v // 2) % 2 for v in pos]
    count = lax.axis_size("box")
    right = (me + 1) % count
    left = (me + count - 1) % count

    def local(src, dst, sem):
        return pltpu.make_async_copy(src, dst, sem)

    def remote(src, dst, ssem, rsem, to):
        return pltpu.make_async_remote_copy(
            src_ref=src, dst_ref=dst, send_sem=ssem, recv_sem=rsem,
            device_id=(to,), device_id_type=MESH,
        )

    def src_copy(c):
        return local(src_h.at[pl.ds(c * CH, CH)], src_v.at[c % SLOTS], l_src.at[c % SLOTS])

    lo, hi = pl.ds(0, R), pl.ds(R, R)
    loads = [[(leaf_h, leaf_v)]]
    loads += [[(stay_h.at[0, 0], w0.at[lo, lo]), (cross_h.at[0, 0], w0.at[lo, hi]),
               (cross_h.at[0, 1], w0.at[hi, lo]), (stay_h.at[0, 1], w0.at[hi, hi])]]
    loads += [[(cross_h.at[1], wl.at[:, :, lo]), (stay_h.at[1], wl.at[:, :, hi])]]
    loads += [[(held.at[2 + 2 * d], w1.at[d, :, lo, at]) for d in range(3) for held, at in ((stay_h, lo), (cross_h, hi))]]
    loads += [[(held.at[3 + 2 * d], w2.at[d, 0, :, :, at]) for d in range(3) for held, at in ((cross_h, lo), (stay_h, hi))]]
    loads += [[(near_h, wo.at[:, pl.ds(0, B + 2 * H)]), (outb_h, wo.at[:, pl.ds(B + 2 * H, R)])]]
    loaded = [leaf_v, w0, wl, w1.at[:, :, lo], w2.at[:, 0], wo]

    def load(i):
        for src, dst in loads[i]:
            local(src, dst, l_w.at[i]).start()

    def load_wait(i):
        local(loaded[i], loaded[i], l_w.at[i]).wait()

    src_copy(0).start()
    for i in range(3):
        load(i)

    barrier = pltpu.get_barrier_semaphore()
    peers = [mate] + a_of + b_of + [left, right]
    for to in peers:
        pl.semaphore_signal(barrier, inc=1, device_id=(to,), device_id_type=MESH)
    pl.semaphore_wait(barrier, len(peers))

    def w_copy(d, b, part):
        some = pl.ds((part % 2) * (R // 2), R // 2)
        there = pl.ds(R + (part % 2) * (R // 2), R // 2)
        src, dst = (
            (stay_h.at[2 + 2 * d, b, some], w1.at[d, b, there, hi]),
            (cross_h.at[2 + 2 * d, b, some], w1.at[d, b, there, lo]),
            (cross_h.at[3 + 2 * d, b, some], w2.at[d, 1, b, some, lo]),
            (stay_h.at[3 + 2 * d, b, some], w2.at[d, 1, b, some, hi]),
        )[part // 2]
        return remote(src, dst, s_w.at[d], r_w.at[d, b], a_of[d])

    for d in range(3):
        for part in range(8):
            w_copy(d, 0, part).start()
    for d in (1, 2):
        for part in range(8):
            w_copy(d, 1, part).start()
    for c in range(1, SLOTS):
        src_copy(c).start()
    for i in range(3, 6):
        load(i)

    @pl.when(me == 0)
    def _():
        for c in range(NC):
            win[c, :, 0:H] = jnp.zeros((CH, H), BF)

    @pl.when(me == count - 1)
    def _():
        for c in range(NC):
            win[c, :, H + 2 * B :] = jnp.zeros((CH, H), BF)

    for i in range(3):
        load_wait(i)

    def one_copy(u):
        return remote(xs1.at[u], xr1.at[u], s_one, r_one.at[u // NC, u % 4], mate)

    def in_copy(d, u):
        return remote(pn.at[d, u, 1 - half[d]], rsw.at[d, u], s_in.at[d], r_in.at[d, u % KEYS], a_of[d])

    def mid_copy(d, u):
        return remote(xs.at[d, u], xr.at[d, u], s_mid.at[d], r_mid.at[d, u % KEYS], b_of[d])

    def back_copy(d, u, mine):
        at = half[d] if mine else 1 - half[d]
        return remote(bs.at[d, u], pn.at[d + 1, u, at], s_back.at[d], r_back.at[d, u % KEYS], a_of[d])

    def halo_copy(side, c):
        if side == 0:
            return remote(
                win.at[c, :, pl.ds(2 * B, H)], win.at[c, :, pl.ds(0, H)], s_halo.at[0], r_halo.at[0, c // 4], right
            )
        return remote(
            win.at[c, :, pl.ds(H, H)], win.at[c, :, pl.ds(H + 2 * B, H)], s_halo.at[1], r_halo.at[1, c // 4], left
        )

    late = ((core == 1) & (pos[0] % 2 == 0), (core == 0) & (pos[0] % 2 == 1))

    def halo_send(c, when):
        for side, there in ((0, me < count - 1), (1, me > 0)):
            chosen = late[side] if when else jnp.logical_not(late[side])

            @pl.when(there & chosen)
            def _(side=side):
                halo_copy(side, c).start()

    def out_copy(u):
        return local(
            obuf.at[u],
            out_h.at[pl.ds((u % NC) * CH, CH), pl.ds(pl.multiple_of((u // NC) * B, B), B)],
            l_out,
        )

    def leaf_stage(c):
        src_copy(c).wait()
        for h in range(2):
            rows = pl.ds(h * HALF, HALF)
            cells = src_v[c % SLOTS, rows, :].astype(BF)
            win[c, rows, H : H + 2 * B] = cells
            p0 = mm(cells[:, :B], leaf_v[0]).astype(BF)
            p1 = mm(cells[:, B:], leaf_v[1]).astype(BF)
            n = mm(jnp.concatenate([p0, p1], axis=1), w0[...]).astype(BF)
            for b in range(2):
                y = mm(n[:, b * R : (b + 1) * R], wl[b])
                xs1[b * NC + c, h] = y[:, :R].astype(BF)
                st1[c % 2, b, h] = y[:, R:]
        one_copy(c).start()
        one_copy(NC + c).start()

        @pl.when(c + SLOTS < NC)
        def _():
            src_copy(c + SLOTS).start()

    def one_stage(c):
        for b in range(2):
            u = b * NC + c
            one_copy(u).wait_recv()
            for h in range(2):
                pn[0, u, h] = (st1[c % 2, b, h] + xr1[u, h].astype(F32)).astype(BF)

        halo_send(c, 0)

        @pl.when(c < AHEAD)
        def _():
            in_copy(0, c).start()

    def in_stage(d, u):
        b = u // NC

        @pl.when(u % NC == 0)
        def _():
            whole = w1.at[d, b]
            remote(whole, whole, s_w.at[d], r_w.at[d, b], a_of[d]).wait_recv()

        if d == 0:

            @pl.when(u + AHEAD < NU)
            def _():
                in_copy(0, u + AHEAD).start()

            for part in range(8):

                @pl.when(u == PIECE_AT[part])
                def _(part=part):
                    w_copy(0, 1, part).start()

        in_copy(d, u).wait_recv()
        pair = jnp.concatenate([pn[d, u, half[d]], rsw[d, u]], axis=1)
        n = mm(pair, w1[d, b]).astype(BF)
        ya = mm(n[:, :R], w2[d, 0, b])
        yb = mm(n[:, R:], w2[d, 1, b])
        xs[d, u, 0] = ya[:, :R].astype(BF)
        xs[d, u, 1] = yb[:, :R].astype(BF)
        mid_copy(d, u).start()
        st[d, u % 4, 0] = ya[:, R:]
        st[d, u % 4, 1] = yb[:, R:]

    def mid_stage(d, u):
        mid_copy(d, u).wait_recv()
        bs[d, u] = (st[d, u % 4, 1] + xr[d, u, 0].astype(F32)).astype(BF)
        back_copy(d, u, True).start()
        pn[d + 1, u, half[d]] = (st[d, u % 4, 0] + xr[d, u, 1].astype(F32)).astype(BF)

    def back_stage(d, u):
        back_copy(d, u, False).wait_recv()
        if d < 2:
            in_copy(d + 1, u).start()

    def out_stage(d, u):
        b = u // NC
        c = u % NC

        some = rsw.at[0, pl.ds(0, NC // 2)]

        @pl.when((u % 4 == 0) & (b == 0) & (me > 0))
        def _():
            remote(some, some, s_halo.at[0], r_halo.at[0, c // 4], right).wait_recv()

        @pl.when((u % 4 == 0) & (b == 1) & (me < count - 1))
        def _():
            remote(some, some, s_halo.at[1], r_halo.at[1, c // 4], left).wait_recv()

        cols = pl.ds(pl.multiple_of(b * B, B), B + 2 * H)
        for h in range(2):
            rows = pl.ds(h * HALF, HALF)
            both = jnp.concatenate([win[c, rows, cols], pn[3, u, h]], axis=1)
            obuf[u, rows, :] = mm(both, wo[b]).astype(BF)
        out_copy(u).start()

    def prologue(i, _):
        @pl.when(i < NC)
        def _():
            leaf_stage(i)

        @pl.when(i > 0)
        def _():
            one_stage(i - 1)

        return 0

    lax.fori_loop(0, NC + 1, prologue, 0)
    for i in range(3, 6):
        load_wait(i)

    bodies = {"in": in_stage, "mid": mid_stage, "back": back_stage}

    def step(t, _):
        for kind, d in STAGES:
            a, b = t - LAG_A[kind][d], t - LAG_B[kind][d]
            u = jnp.where(a < FIRST, a, b)

            @pl.when((a >= 0) & ((a < FIRST) | (b >= FIRST)) & (u < NU))
            def _(u=u, kind=kind, d=d):
                bodies[kind](d, u)

        def outs(t):
            a, b = t + 1 - LAG_A["back"][2], t + 1 - LAG_B["back"][2]
            came = jnp.where(a < FIRST, a, jnp.maximum(b, FIRST))
            return jnp.clip(jnp.minimum(came, OUT_RATE * (t - OUT_AT + 1)), 0, NU)

        def result(u, _):
            out_stage(2, u)
            return 0

        lax.fori_loop(outs(t - 1), outs(t), result, 0)

        @pl.when((t >= HALO_AT) & (t < HALO_AT + 2))
        def _():
            for k in range(4):
                halo_send(4 * (t - HALO_AT) + k, 1)

        return 0

    lax.fori_loop(0, STEPS, step, 0)

    local(obuf, obuf, l_out).wait()
    remote(xs1, xr1, s_one, r_one.at[0, 0], mate).wait_send()
    for d in range(3):
        remote(rsw.at[d], rsw.at[d], s_in.at[d], r_in.at[d, 0], a_of[d]).wait_send()
        remote(xs.at[d], xr.at[d], s_mid.at[d], r_mid.at[d, 0], b_of[d]).wait_send()
        remote(bs.at[d], bs.at[d], s_back.at[d], r_back.at[d, 0], a_of[d]).wait_send()
        remote(w1.at[d], w1.at[d], s_w.at[d], r_w.at[d, 0], a_of[d]).wait_send()
    whole = rsw.at[0, pl.ds(0, NC)]

    @pl.when(me < count - 1)
    def _():
        remote(whole, whole, s_halo.at[0], r_halo.at[0, 0], right).wait_send()

    @pl.when(me > 0)
    def _():
        remote(whole, whole, s_halo.at[1], r_halo.at[1, 0], left).wait_send()


def widen_kernel(x_h, o_h, x_v, o_v, l_in, l_out):
    parts = NV // WROWS

    def get(i):
        return pltpu.make_async_copy(x_h.at[pl.ds(i * WROWS, WROWS)], x_v.at[i], l_in.at[i])

    def put(i):
        return pltpu.make_async_copy(o_v.at[i], o_h.at[pl.ds(i * WROWS, WROWS)], l_out.at[i])

    for i in range(parts):
        get(i).start()
    for i in range(parts):
        get(i).wait()
        o_v[i] = x_v[i].astype(F32)
        put(i).start()
    for i in range(parts):
        put(i).wait()


def widen(x):
    parts = NV // WROWS
    spec = pl.BlockSpec(memory_space=pl.ANY)
    return pl.pallas_call(
        widen_kernel, in_specs=[spec], out_specs=spec,
        out_shape=jax.ShapeDtypeStruct((NV, 2 * B), F32),
        scratch_shapes=[
            pltpu.VMEM((parts, WROWS, 2 * B), BF), pltpu.VMEM((parts, WROWS, 2 * B), F32),
            pltpu.SemaphoreType.DMA((parts,)), pltpu.SemaphoreType.DMA((parts,)),
        ],
        compiler_params=pltpu.CompilerParams(vmem_limit_bytes=60_000_000),
    )(x)


def per_device(sources, leaf_basis, stay_blocks, cross_blocks, out_basis, near_blocks):
    dma = pltpu.SemaphoreType.DMA
    v = pltpu.VMEM
    scratch = [
        v((SLOTS, CH, 2 * B), F32),
        v(leaf_basis.shape, BF),
        v((2 * R, 2 * R), BF),
        v((2, R, 2 * R), BF),
        v((3, 2, 2 * R, 2 * R), BF),
        v((3, 2, 2, R, 2 * R), BF),
        v((2, B + 2 * H + R, B), BF),
        v((NC, CH, 2 * B + 2 * H), BF),
        v((NU, 2, HALF, R), BF),
        v((NU, 2, HALF, R), BF),
        v((2, 2, 2, HALF, R), F32),
        v((4, NU, 2, HALF, R), BF),
        v((3, NU, HALF, R), BF),
        v((3, 4, 2, HALF, R), F32),
        v((3, NU, 2, HALF, R), BF),
        v((3, NU, 2, HALF, R), BF),
        v((3, NU, HALF, R), BF),
        v((NU, CH, B), BF),
        dma((SLOTS,)), dma((6,)), dma,
        dma((2, 4)), dma((3, KEYS)), dma((3, KEYS)), dma((3, KEYS)), dma((2, 2)), dma((3, 2)),
        dma, dma((3,)), dma((3,)), dma((3,)), dma((2,)), dma((3,)),
    ]
    out = pl.pallas_call(
        kernel,
        out_shape=jax.ShapeDtypeStruct((NV, 2 * B), BF),
        in_specs=[pl.BlockSpec(memory_space=pl.ANY)] * 6,
        out_specs=pl.BlockSpec(memory_space=pl.ANY),
        scratch_shapes=scratch,
        compiler_params=pltpu.CompilerParams(
            collective_id=0, has_side_effects=True, vmem_limit_bytes=66_900_000
        ),
    )(sources, leaf_basis, stay_blocks, cross_blocks, out_basis, near_blocks)
    return widen(out)


def solution(mesh):
    in_specs = (
        P(None, "box"),
        P("box", None, None),
        P(None, "box", None, None),
        P(None, "box", None, None),
        P("box", None, None),
        P("box", None, None),
    )
    return jax.shard_map(
        per_device, mesh=mesh, in_specs=in_specs, out_specs=P(None, "box"), check_vma=False
    )
```

```python
import jax
import jax.numpy as jnp
from jax import lax
from jax.experimental import pallas as pl
from jax.experimental.pallas import tpu as pltpu
from jax.sharding import PartitionSpec as P

MESH = pl.DeviceIdType.MESH
BF = jnp.bfloat16
F32 = jnp.float32

B = 512
H = 128
R = 256
NV = 2048
CH = 256
NC = NV // CH
NU = 2 * NC
HALF = CH // 2
SLOTS = 4

STRIDE = (2, 8, 32)
AHEAD = 3
BEFORE = AHEAD + 1
STAGES = (("in", 0), ("mid", 0), ("back", 0), ("in", 1), ("mid", 1), ("back", 1), ("in", 2), ("mid", 2), ("back", 2))
FIRST = 8
AT_A = (0, 2, 4, 5, 7, 9, 10, 12, 14)
AT_B = (0, 2, 4, 5, 7, 9, 10, 12, 14)
LAG_A = dict(zip(("in", "mid", "back"), (AT_A[0::3], AT_A[1::3], AT_A[2::3])))
LAG_B = dict(zip(("in", "mid", "back"), (AT_B[0::3], AT_B[1::3], AT_B[2::3])))
OUT_LAG = 1
STEPS = NU + LAG_B["back"][2] + OUT_LAG
HALO_AT = NU + 1
OUT_AT = HALO_AT + 2
OUT_RATE = 3
PAIR_AT = 0
PIECE_AT = (0, 0, 0, 0, 1, 1, 1, 1)
KEYS = 8
WROWS = 128


def mm(a, b):
    return jnp.dot(a, b, preferred_element_type=F32)


def kernel(
    src_h, leaf_h, stay_h, cross_h, outb_h, near_h, out_h,
    src_v, leaf_v, w0, wl, w1, w2, wo, win, n1, xr1, pn, rsw, st, xs, xr, bs, fin, obuf,
    l_src, l_w, l_out,
    r_one, r_in, r_mid, r_back, r_halo, r_w, r_pair, r_level, r_fin,
    s_one, s_in, s_mid, s_back, s_halo, s_w, s_pair, s_level, s_pass, s_fin,
):
    me = lax.axis_index("box")
    core = me % 2
    mate = me + 1 - 2 * core
    pos = [(me // st) % 4 for st in STRIDE]
    a_of = [me + (1 - 2 * (v % 2)) * st for v, st in zip(pos, STRIDE)]
    b_of = [me + (3 - 2 * v) * st for v, st in zip(pos, STRIDE)]
    half = [(v % 2 + v // 2) % 2 for v in pos]
    count = lax.axis_size("box")
    right = (me + 1) % count
    left = (me + count - 1) % count

    def local(src, dst, sem):
        return pltpu.make_async_copy(src, dst, sem)

    def remote(src, dst, ssem, rsem, to):
        return pltpu.make_async_remote_copy(
            src_ref=src, dst_ref=dst, send_sem=ssem, recv_sem=rsem,
            device_id=(to,), device_id_type=MESH,
        )

    def src_start(c):
        for h in range(2):
            rows = pl.ds(h * (NV // 2) + c * HALF, HALF)
            local(src_h.at[rows], src_v.at[c % SLOTS, pl.ds(h * HALF, HALF)], l_src.at[c % SLOTS]).start()

    def src_wait(c):
        local(src_v.at[c % SLOTS], src_v.at[c % SLOTS], l_src.at[c % SLOTS]).wait()

    keep = [core == h for h in half]
    lo, hi = pl.ds(0, R), pl.ds(R, R)
    loads = [[(leaf_h, leaf_v)]]
    loads += [[(stay_h.at[0, 0], w0.at[lo, lo]), (cross_h.at[0, 0], w0.at[lo, hi]),
               (cross_h.at[0, 1], w0.at[hi, lo]), (stay_h.at[0, 1], w0.at[hi, hi])]]
    loads += [[(stay_h.at[1], wl.at[:, lo, lo]), (cross_h.at[1], wl.at[:, lo, hi])]]
    loads += [[(near_h, wo.at[:, pl.ds(0, B + 2 * H)]), (outb_h, wo.at[:, pl.ds(B + 2 * H, R)])]]
    loaded = [leaf_v, w0, wl.at[:, lo], wo]

    def load(i):
        for src, dst in loads[i]:
            local(src, dst, l_w.at[i]).start()

    def load_wait(i):
        local(loaded[i], loaded[i], l_w.at[i]).wait()

    src_start(0)
    for i in range(3):
        load(i)

    barrier = pltpu.get_barrier_semaphore()
    other_of = [a + 1 - 2 * core for a in a_of]
    peers = [mate] + a_of + other_of[1:] + b_of + [left, right]
    for to in peers:
        pl.semaphore_signal(barrier, inc=1, device_id=(to,), device_id_type=MESH)
    pl.semaphore_wait(barrier, len(peers))

    def w_copy(d, b, part, to):
        some = pl.ds((part % 2) * (R // 2), R // 2)
        there = pl.ds(R + (part % 2) * (R // 2), R // 2)
        src, dst = (
            (stay_h.at[2 + 2 * d, b, some], w1.at[d, b, there, hi]),
            (cross_h.at[2 + 2 * d, b, some], w1.at[d, b, there, lo]),
            (cross_h.at[3 + 2 * d, b, some], w2.at[d, 1, b, some, lo]),
            (stay_h.at[3 + 2 * d, b, some], w2.at[d, 1, b, some, hi]),
        )[part // 2]
        return remote(src, dst, s_w.at[d], r_w.at[d, b], to)

    def pair_blocks(d):
        return (
            (stay_h.at[2 + 2 * d], w1.at[d, :, lo, lo]),
            (cross_h.at[2 + 2 * d], w1.at[d, :, lo, hi]),
            (cross_h.at[3 + 2 * d], w2.at[d, 0, :, :, lo]),
            (stay_h.at[3 + 2 * d], w2.at[d, 0, :, :, hi]),
        )

    def pass_on(b):
        for ref in (w1.at[0, b, hi], w2.at[0, 1, b]):
            remote(ref, ref, s_pass, r_w.at[0, b], mate).start()

    def w_wait(d, b):
        whole = w1.at[d, b]
        remote(whole, whole, s_w.at[d], r_w.at[d, b], mate).wait_recv()

    @pl.when(jnp.logical_not(keep[0]))
    def _():
        for part in range(8):
            w_copy(0, 0, part, a_of[0]).start()

    for src, dst in ((stay_h.at[1], wl.at[:, hi, hi]), (cross_h.at[1], wl.at[:, hi, lo])):
        remote(src, dst, s_level, r_level, mate).start()
    def pair_start(d):
        @pl.when(keep[d])
        def _():
            for src, dst in pair_blocks(d):
                local(src, dst, l_w.at[4 + d]).start()
                remote(src, dst, s_pair.at[d], r_pair.at[d], mate).start()

    def pair_wait(d):
        @pl.when(keep[d])
        def _():
            local(w1.at[d], w1.at[d], l_w.at[4 + d]).wait()

        @pl.when(jnp.logical_not(keep[d]))
        def _():
            remote(w1.at[d], w1.at[d], s_pair.at[d], r_pair.at[d], mate).wait_recv()

    for d in (1, 2):

        @pl.when(jnp.logical_not(keep[d]))
        def _(d=d):
            for to in (a_of[d], other_of[d]):
                for src, dst in (
                    (stay_h.at[2 + 2 * d], w1.at[d, :, hi, hi]),
                    (cross_h.at[2 + 2 * d], w1.at[d, :, hi, lo]),
                    (cross_h.at[3 + 2 * d], w2.at[d, 1, :, :, lo]),
                    (stay_h.at[3 + 2 * d], w2.at[d, 1, :, :, hi]),
                ):
                    remote(src, dst, s_w.at[d], r_w.at[d, 0], to).start()

    for c in range(1, SLOTS):
        src_start(c)
    load(3)

    @pl.when(me == 0)
    def _():
        for c in range(NC):
            win[c, :, 0:H] = jnp.zeros((CH, H), BF)

    @pl.when(me == count - 1)
    def _():
        for c in range(NC):
            win[c, :, H + 2 * B :] = jnp.zeros((CH, H), BF)

    for i in range(3):
        load_wait(i)
    remote(wl.at[:, hi], wl.at[:, hi], s_level, r_level, mate).wait_recv()

    def one_copy(u):
        return remote(n1.at[u, 1 - core], xr1.at[u], s_one, r_one.at[u // NC, u % 4], mate)

    def in_copy(d, u):
        return remote(pn.at[d, u, 1 - half[d]], rsw.at[d, u], s_in.at[d], r_in.at[d, u % KEYS], a_of[d])

    def mid_copy(d, u):
        return remote(xs.at[d, u], xr.at[d, u], s_mid.at[d], r_mid.at[d, u % KEYS], b_of[d])

    def back_copy(d, u, mine):
        at = half[d] if mine else 1 - half[d]
        return remote(bs.at[d, u], pn.at[d + 1, u, at], s_back.at[d], r_back.at[d, u % KEYS], a_of[d])

    def fin_copy(u):
        return remote(pn.at[3, u, 1 - core], fin.at[u], s_fin, r_fin.at[u], mate)

    def halo_copy(side, c):
        if side == 0:
            return remote(
                win.at[c, :, pl.ds(2 * B, H)], win.at[c, :, pl.ds(0, H)], s_halo.at[0], r_halo.at[0, c // 4], right
            )
        return remote(
            win.at[c, :, pl.ds(H, H)], win.at[c, :, pl.ds(H + 2 * B, H)], s_halo.at[1], r_halo.at[1, c // 4], left
        )

    late = ((core == 1) & (pos[0] % 2 == 0), (core == 0) & (pos[0] % 2 == 1))

    def halo_send(c, when):
        for side, there in ((0, me < count - 1), (1, me > 0)):
            chosen = late[side] if when else jnp.logical_not(late[side])

            @pl.when(there & chosen)
            def _(side=side):
                halo_copy(side, c).start()

    def out_copy(u, h):
        rows = pl.ds(h * (NV // 2) + (u % NC) * HALF, HALF)
        cols = pl.ds(pl.multiple_of((u // NC) * B, B), B)
        return local(obuf.at[u, pl.ds(h * HALF, HALF)], out_h.at[rows, cols], l_out)

    def leaf_stage(c):
        src_wait(c)
        for h in range(2):
            rows = pl.ds(h * HALF, HALF)
            cells = src_v[c % SLOTS, rows, :].astype(BF)
            win[c, rows, H : H + 2 * B] = cells
            p0 = mm(cells[:, :B], leaf_v[0]).astype(BF)
            p1 = mm(cells[:, B:], leaf_v[1]).astype(BF)
            n = mm(jnp.concatenate([p0, p1], axis=1), w0[...]).astype(BF)
            n1[c, h] = n[:, :R]
            n1[NC + c, h] = n[:, R:]
        one_copy(c).start()
        one_copy(NC + c).start()

        @pl.when(c + SLOTS < NC)
        def _():
            src_start(c + SLOTS)

    def one_stage(c):
        for b in range(2):
            u = b * NC + c
            one_copy(u).wait_recv()
            pair = jnp.concatenate([n1[u, core], xr1[u]], axis=1)
            p = mm(pair, wl[b]).astype(BF)
            pn[0, u, core] = p[:, :R]
            pn[0, u, 1 - core] = p[:, R:]

        halo_send(c, 0)

        in_copy(0, c).start()

    def in_stage(d, u):
        b = u // NC

        if d == 0:

            @pl.when((u % NC == 0) & jnp.logical_not(keep[0]))
            def _():
                w_wait(0, b)

            @pl.when(u == 2)
            def _():
                pair_start(2)

            @pl.when((u == NC - 2) & keep[0])
            def _():
                w_wait(0, 1)
                pass_on(1)

        else:

            @pl.when(u == 0)
            def _():
                pair_wait(d)
                remote(w1.at[d], w1.at[d], s_w.at[d], r_w.at[d, 0], mate).wait_recv()

        if d == 0:

            @pl.when((u + AHEAD >= NC) & (u + AHEAD < NU))
            def _():
                in_copy(0, u + AHEAD).start()

            for part in range(8):

                @pl.when((u == PIECE_AT[part]) & jnp.logical_not(keep[0]))
                def _(part=part):
                    w_copy(0, 1, part, a_of[0]).start()

        in_copy(d, u).wait_recv()
        pair = jnp.concatenate([pn[d, u, half[d]], rsw[d, u]], axis=1)
        n = mm(pair, w1[d, b]).astype(BF)
        ya = mm(n[:, :R], w2[d, 0, b])
        yb = mm(n[:, R:], w2[d, 1, b])
        xs[d, u, 0] = ya[:, :R].astype(BF)
        xs[d, u, 1] = yb[:, :R].astype(BF)
        mid_copy(d, u).start()
        st[d, u % 4, 0] = ya[:, R:]
        st[d, u % 4, 1] = yb[:, R:]

    def mid_stage(d, u):
        mid_copy(d, u).wait_recv()
        bs[d, u] = (st[d, u % 4, 1] + xr[d, u, 0].astype(F32)).astype(BF)
        back_copy(d, u, True).start()
        pn[d + 1, u, half[d]] = (st[d, u % 4, 0] + xr[d, u, 1].astype(F32)).astype(BF)

    def back_stage(d, u):
        back_copy(d, u, False).wait_recv()
        if d < 2:
            in_copy(d + 1, u).start()
        else:
            fin_copy(u).start()

    def out_stage(d, u):
        b = u // NC
        c = u % NC

        some = rsw.at[0, pl.ds(0, NC // 2)]

        @pl.when((u % 4 == 0) & (b == 0) & (me > 0))
        def _():
            remote(some, some, s_halo.at[0], r_halo.at[0, c // 4], right).wait_recv()

        @pl.when((u % 4 == 0) & (b == 1) & (me < count - 1))
        def _():
            remote(some, some, s_halo.at[1], r_halo.at[1, c // 4], left).wait_recv()

        fin_copy(u).wait_recv()
        cols = pl.ds(pl.multiple_of(b * B, B), B + 2 * H)
        for at, proxy in ((core, pn[3, u, core]), (1 - core, fin[u])):
            rows = pl.ds(pl.multiple_of(at * HALF, HALF), HALF)
            both = jnp.concatenate([win[c, rows, cols], proxy], axis=1)
            obuf[u, rows, :] = mm(both, wo[b]).astype(BF)
        for h in range(2):
            out_copy(u, h).start()

    def begin(i):
        @pl.when(i < NC)
        def _():
            leaf_stage(i)

            @pl.when(i == PAIR_AT)
            def _():
                pair_start(0)

        @pl.when((i > 0) & (i <= NC))
        def _():
            one_stage(i - 1)

    def prologue(i, _):
        begin(i)
        return 0

    lax.fori_loop(0, BEFORE, prologue, 0)
    load_wait(3)
    pair_wait(0)

    @pl.when(keep[0])
    def _():
        w_wait(0, 0)
        pass_on(0)

    pair_start(1)

    bodies = {"in": in_stage, "mid": mid_stage, "back": back_stage}

    def step(t, _):
        begin(t + BEFORE)
        for kind, d in STAGES:
            a, b = t - LAG_A[kind][d], t - LAG_B[kind][d]
            u = jnp.where(a < FIRST, a, b)

            @pl.when((a >= 0) & ((a < FIRST) | (b >= FIRST)) & (u < NU))
            def _(u=u, kind=kind, d=d):
                bodies[kind](d, u)

        def outs(t):
            a, b = t + 1 - OUT_LAG - LAG_A["back"][2], t + 1 - OUT_LAG - LAG_B["back"][2]
            came = jnp.where(a < FIRST, a, jnp.maximum(b, FIRST))
            return jnp.clip(jnp.minimum(came, OUT_RATE * (t - OUT_AT + 1)), 0, NU)

        def result(u, _):
            out_stage(2, u)
            return 0

        lax.fori_loop(outs(t - 1), outs(t), result, 0)

        @pl.when((t >= HALO_AT) & (t < HALO_AT + 2))
        def _():
            for k in range(4):
                halo_send(4 * (t - HALO_AT) + k, 1)

        return 0

    lax.fori_loop(0, STEPS, step, 0)

    local(obuf, obuf, l_out).wait()
    remote(xr1, xr1, s_one, r_one.at[0, 0], mate).wait_send()
    for d in range(3):
        remote(rsw.at[d], rsw.at[d], s_in.at[d], r_in.at[d, 0], a_of[d]).wait_send()
        remote(xs.at[d], xr.at[d], s_mid.at[d], r_mid.at[d, 0], b_of[d]).wait_send()
        remote(bs.at[d], bs.at[d], s_back.at[d], r_back.at[d, 0], a_of[d]).wait_send()
        sent = w1.at[0] if d == 0 else w1.at[pl.ds(0, 2)]

        @pl.when(keep[d])
        def _(d=d):
            remote(w1.at[d], w1.at[d], s_pair.at[d], r_pair.at[d], mate).wait_send()

        @pl.when(jnp.logical_not(keep[d]))
        def _(d=d, sent=sent):
            remote(sent, sent, s_w.at[d], r_w.at[d, 0], a_of[d]).wait_send()

    @pl.when(keep[0])
    def _():
        remote(w1.at[0], w1.at[0], s_pass, r_w.at[0, 0], mate).wait_send()

    remote(wl.at[:, hi], wl.at[:, hi], s_level, r_level, mate).wait_send()
    remote(fin, fin, s_fin, r_fin.at[0], mate).wait_send()
    whole = rsw.at[0, pl.ds(0, NC)]

    @pl.when(me < count - 1)
    def _():
        remote(whole, whole, s_halo.at[0], r_halo.at[0, 0], right).wait_send()

    @pl.when(me > 0)
    def _():
        remote(whole, whole, s_halo.at[1], r_halo.at[1, 0], left).wait_send()


def widen_kernel(x_h, o_h, x_v, o_v, l_in, l_out):
    parts = NV // WROWS

    def get(i):
        return pltpu.make_async_copy(x_h.at[pl.ds(i * WROWS, WROWS)], x_v.at[i], l_in.at[i])

    def put(i):
        return pltpu.make_async_copy(o_v.at[i], o_h.at[pl.ds(i * WROWS, WROWS)], l_out.at[i])

    for i in range(parts):
        get(i).start()
    for i in range(parts):
        get(i).wait()
        o_v[i] = x_v[i].astype(F32)
        put(i).start()
    for i in range(parts):
        put(i).wait()


def widen(x):
    parts = NV // WROWS
    spec = pl.BlockSpec(memory_space=pl.ANY)
    return pl.pallas_call(
        widen_kernel, in_specs=[spec], out_specs=spec,
        out_shape=jax.ShapeDtypeStruct((NV, 2 * B), F32),
        scratch_shapes=[
            pltpu.VMEM((parts, WROWS, 2 * B), BF), pltpu.VMEM((parts, WROWS, 2 * B), F32),
            pltpu.SemaphoreType.DMA((parts,)), pltpu.SemaphoreType.DMA((parts,)),
        ],
        compiler_params=pltpu.CompilerParams(vmem_limit_bytes=60_000_000),
    )(x)


def per_device(sources, leaf_basis, stay_blocks, cross_blocks, out_basis, near_blocks):
    dma = pltpu.SemaphoreType.DMA
    v = pltpu.VMEM
    scratch = [
        v((SLOTS, CH, 2 * B), F32),
        v(leaf_basis.shape, BF),
        v((2 * R, 2 * R), BF),
        v((2, 2 * R, 2 * R), BF),
        v((3, 2, 2 * R, 2 * R), BF),
        v((3, 2, 2, R, 2 * R), BF),
        v((2, B + 2 * H + R, B), BF),
        v((NC, CH, 2 * B + 2 * H), BF),
        v((NU, 2, HALF, R), BF),
        v((NU, HALF, R), BF),
        v((4, NU, 2, HALF, R), BF),
        v((3, NU, HALF, R), BF),
        v((3, 4, 2, HALF, R), F32),
        v((3, NU, 2, HALF, R), BF),
        v((3, NU, 2, HALF, R), BF),
        v((3, NU, HALF, R), BF),
        v((NU, HALF, R), BF),
        v((NU, CH, B), BF),
        dma((SLOTS,)), dma((7,)), dma,
        dma((2, 4)), dma((3, KEYS)), dma((3, KEYS)), dma((3, KEYS)), dma((2, 2)), dma((3, 2)), dma((3,)), dma, dma((NU,)),
        dma, dma((3,)), dma((3,)), dma((3,)), dma((2,)), dma((3,)), dma((3,)), dma, dma, dma,
    ]
    out = pl.pallas_call(
        kernel,
        out_shape=jax.ShapeDtypeStruct((NV, 2 * B), BF),
        in_specs=[pl.BlockSpec(memory_space=pl.ANY)] * 6,
        out_specs=pl.BlockSpec(memory_space=pl.ANY),
        scratch_shapes=scratch,
        compiler_params=pltpu.CompilerParams(
            collective_id=0, has_side_effects=True, vmem_limit_bytes=66_900_000
        ),
    )(sources, leaf_basis, stay_blocks, cross_blocks, out_basis, near_blocks)
    return widen(out)


def solution(mesh):
    in_specs = (
        P(None, "box"),
        P("box", None, None),
        P(None, "box", None, None),
        P(None, "box", None, None),
        P("box", None, None),
        P("box", None, None),
    )
    return jax.shard_map(
        per_device, mesh=mesh, in_specs=in_specs, out_specs=P(None, "box"), check_vma=False
    )
```

```python
import jax
import jax.numpy as jnp
from jax import lax
from jax.experimental import pallas as pl
from jax.experimental.pallas import tpu as pltpu
from jax.sharding import PartitionSpec as P

MESH = pl.DeviceIdType.MESH
BF = jnp.bfloat16
F32 = jnp.float32

B = 512
H = 128
R = 256
NV = 2048
CH = 256
NC = NV // CH
NU = 2 * NC
HALF = CH // 2
SLOTS = 4

STRIDE = (2, 8, 32)
AHEAD = 2
BEFORE = AHEAD + 1
STAGES = (("back", 0), ("back", 1), ("back", 2), ("in", 0), ("mid", 0), ("in", 1), ("mid", 1), ("in", 2), ("mid", 2))
FIRST = 8
AT_A = (0, 2, 4, 5, 7, 9, 10, 12, 14)
AT_B = (0, 2, 4, 5, 7, 9, 10, 12, 14)
LAG_A = dict(zip(("in", "mid", "back"), (AT_A[0::3], AT_A[1::3], AT_A[2::3])))
LAG_B = dict(zip(("in", "mid", "back"), (AT_B[0::3], AT_B[1::3], AT_B[2::3])))
OUT_LAG = 1
STEPS = NU + LAG_B["back"][2] + OUT_LAG
HALO_AT = NU + 1
OUT_AT = HALO_AT + 2
OUT_RATE = 3
PAIR_AT = 0
PIECE_AT = (2, 2, 3, 3, 4, 4, 5, 5)
KEYS = 8
WROWS = 128


def mm(a, b):
    return jnp.dot(a, b, preferred_element_type=F32)


def kernel(
    src_h, leaf_h, stay_h, cross_h, outb_h, near_h, out_h,
    src_v, leaf_v, w0, wl, w1, w2, wo, win, n1, xr1, pn, rsw, st, xs, xr, bs, fin, obuf,
    l_src, l_w, l_out,
    r_one, r_in, r_mid, r_back, r_halo, r_w, r_pair, r_level, r_fin,
    s_one, s_in, s_mid, s_back, s_halo, s_w, s_pair, s_level, s_pass, s_fin,
):
    me = lax.axis_index("box")
    core = me % 2
    mate = me + 1 - 2 * core
    pos = [(me // st) % 4 for st in STRIDE]
    a_of = [me + (1 - 2 * (v % 2)) * st for v, st in zip(pos, STRIDE)]
    b_of = [me + (3 - 2 * v) * st for v, st in zip(pos, STRIDE)]
    half = [(v % 2 + v // 2) % 2 for v in pos]
    count = lax.axis_size("box")
    right = (me + 1) % count
    left = (me + count - 1) % count

    def local(src, dst, sem):
        return pltpu.make_async_copy(src, dst, sem)

    def remote(src, dst, ssem, rsem, to):
        return pltpu.make_async_remote_copy(
            src_ref=src, dst_ref=dst, send_sem=ssem, recv_sem=rsem,
            device_id=(to,), device_id_type=MESH,
        )

    def src_start(c):
        for h in range(2):
            rows = pl.ds(h * (NV // 2) + c * HALF, HALF)
            local(src_h.at[rows], src_v.at[c % SLOTS, pl.ds(h * HALF, HALF)], l_src.at[c % SLOTS]).start()

    def src_wait(c):
        local(src_v.at[c % SLOTS], src_v.at[c % SLOTS], l_src.at[c % SLOTS]).wait()

    keep = [core == h for h in half]
    lo, hi = pl.ds(0, R), pl.ds(R, R)
    loads = [[(leaf_h, leaf_v)]]
    loads += [[(stay_h.at[0, 0], w0.at[lo, lo]), (cross_h.at[0, 0], w0.at[lo, hi]),
               (cross_h.at[0, 1], w0.at[hi, lo]), (stay_h.at[0, 1], w0.at[hi, hi])]]
    loads += [[(stay_h.at[1], wl.at[:, lo, lo]), (cross_h.at[1], wl.at[:, lo, hi])]]
    loads += [[(near_h, wo.at[:, pl.ds(0, B + 2 * H)]), (outb_h, wo.at[:, pl.ds(B + 2 * H, R)])]]
    loaded = [leaf_v, w0, wl.at[:, lo], wo]

    def load(i):
        for src, dst in loads[i]:
            local(src, dst, l_w.at[i]).start()

    def load_wait(i):
        local(loaded[i], loaded[i], l_w.at[i]).wait()

    src_start(0)
    for i in range(3):
        load(i)

    barrier = pltpu.get_barrier_semaphore()
    other_of = [a + 1 - 2 * core for a in a_of]
    peers = [mate] + a_of + other_of[1:] + b_of + [left, right]
    for to in peers:
        pl.semaphore_signal(barrier, inc=1, device_id=(to,), device_id_type=MESH)
    pl.semaphore_wait(barrier, len(peers))

    def w_copy(d, b, part, to):
        some = pl.ds((part % 2) * (R // 2), R // 2)
        there = pl.ds(R + (part % 2) * (R // 2), R // 2)
        src, dst = (
            (stay_h.at[2 + 2 * d, b, some], w1.at[d, b, there, hi]),
            (cross_h.at[2 + 2 * d, b, some], w1.at[d, b, there, lo]),
            (cross_h.at[3 + 2 * d, b, some], w2.at[d, 1, b, some, lo]),
            (stay_h.at[3 + 2 * d, b, some], w2.at[d, 1, b, some, hi]),
        )[part // 2]
        return remote(src, dst, s_w.at[d], r_w.at[d, b], to)

    def pair_blocks(d):
        return (
            (stay_h.at[2 + 2 * d], w1.at[d, :, lo, lo]),
            (cross_h.at[2 + 2 * d], w1.at[d, :, lo, hi]),
            (cross_h.at[3 + 2 * d], w2.at[d, 0, :, :, lo]),
            (stay_h.at[3 + 2 * d], w2.at[d, 0, :, :, hi]),
        )

    def pass_on(b):
        for ref in (w1.at[0, b, hi], w2.at[0, 1, b]):
            remote(ref, ref, s_pass, r_w.at[0, b], mate).start()

    def w_wait(d, b):
        whole = w1.at[d, b]
        remote(whole, whole, s_w.at[d], r_w.at[d, b], mate).wait_recv()

    @pl.when(jnp.logical_not(keep[0]))
    def _():
        for part in range(8):
            w_copy(0, 0, part, a_of[0]).start()

    for src, dst in ((stay_h.at[1], wl.at[:, hi, hi]), (cross_h.at[1], wl.at[:, hi, lo])):
        remote(src, dst, s_level, r_level, mate).start()
    def pair_start(d):
        @pl.when(keep[d])
        def _():
            for src, dst in pair_blocks(d):
                local(src, dst, l_w.at[4 + d]).start()
                remote(src, dst, s_pair.at[d], r_pair.at[d], mate).start()

    def pair_wait(d):
        @pl.when(keep[d])
        def _():
            local(w1.at[d], w1.at[d], l_w.at[4 + d]).wait()

        @pl.when(jnp.logical_not(keep[d]))
        def _():
            remote(w1.at[d], w1.at[d], s_pair.at[d], r_pair.at[d], mate).wait_recv()

    for d in (1, 2):

        @pl.when(jnp.logical_not(keep[d]))
        def _(d=d):
            for to in (a_of[d], other_of[d]):
                for src, dst in (
                    (stay_h.at[2 + 2 * d], w1.at[d, :, hi, hi]),
                    (cross_h.at[2 + 2 * d], w1.at[d, :, hi, lo]),
                    (cross_h.at[3 + 2 * d], w2.at[d, 1, :, :, lo]),
                    (stay_h.at[3 + 2 * d], w2.at[d, 1, :, :, hi]),
                ):
                    remote(src, dst, s_w.at[d], r_w.at[d, 0], to).start()

    for c in range(1, SLOTS):
        src_start(c)
    load(3)

    @pl.when(me == 0)
    def _():
        for c in range(NC):
            win[c, :, 0:H] = jnp.zeros((CH, H), BF)

    @pl.when(me == count - 1)
    def _():
        for c in range(NC):
            win[c, :, H + 2 * B :] = jnp.zeros((CH, H), BF)

    for i in range(3):
        load_wait(i)
    remote(wl.at[:, hi], wl.at[:, hi], s_level, r_level, mate).wait_recv()

    def one_copy(u):
        return remote(n1.at[u, 1 - core], xr1.at[u], s_one, r_one.at[u // NC, u % 4], mate)

    def in_copy(d, u):
        return remote(pn.at[d, u, 1 - half[d]], rsw.at[d, u], s_in.at[d], r_in.at[d, u % KEYS], a_of[d])

    def mid_copy(d, u):
        return remote(xs.at[d, u], xr.at[d, u], s_mid.at[d], r_mid.at[d, u % KEYS], b_of[d])

    def back_copy(d, u, mine):
        at = half[d] if mine else 1 - half[d]
        return remote(bs.at[d, u], pn.at[d + 1, u, at], s_back.at[d], r_back.at[d, u % KEYS], a_of[d])

    def fin_copy(u):
        return remote(pn.at[3, u, 1 - core], fin.at[u], s_fin, r_fin.at[u], mate)

    def halo_copy(side, c):
        if side == 0:
            return remote(
                win.at[c, :, pl.ds(2 * B, H)], win.at[c, :, pl.ds(0, H)], s_halo.at[0], r_halo.at[0, c // 4], right
            )
        return remote(
            win.at[c, :, pl.ds(H, H)], win.at[c, :, pl.ds(H + 2 * B, H)], s_halo.at[1], r_halo.at[1, c // 4], left
        )

    late = ((core == 1) & (pos[0] % 2 == 0), (core == 0) & (pos[0] % 2 == 1))

    def halo_send(c, when):
        for side, there in ((0, me < count - 1), (1, me > 0)):
            chosen = late[side] if when else jnp.logical_not(late[side])

            @pl.when(there & chosen)
            def _(side=side):
                halo_copy(side, c).start()

    def out_copy(u, h):
        rows = pl.ds(h * (NV // 2) + (u % NC) * HALF, HALF)
        cols = pl.ds(pl.multiple_of((u // NC) * B, B), B)
        return local(obuf.at[u, pl.ds(h * HALF, HALF)], out_h.at[rows, cols], l_out)

    def leaf_stage(c):
        src_wait(c)
        for h in range(2):
            rows = pl.ds(h * HALF, HALF)
            cells = src_v[c % SLOTS, rows, :].astype(BF)
            win[c, rows, H : H + 2 * B] = cells
            p0 = mm(cells[:, :B], leaf_v[0]).astype(BF)
            p1 = mm(cells[:, B:], leaf_v[1]).astype(BF)
            n = mm(jnp.concatenate([p0, p1], axis=1), w0[...]).astype(BF)
            n1[c, h] = n[:, :R]
            n1[NC + c, h] = n[:, R:]
        one_copy(c).start()
        one_copy(NC + c).start()

        @pl.when(c + SLOTS < NC)
        def _():
            src_start(c + SLOTS)

    def one_stage(c):
        for b in range(2):
            u = b * NC + c
            one_copy(u).wait_recv()
            pair = jnp.concatenate([n1[u, core], xr1[u]], axis=1)
            p = mm(pair, wl[b]).astype(BF)
            pn[0, u, core] = p[:, :R]
            pn[0, u, 1 - core] = p[:, R:]

        halo_send(c, 0)

        in_copy(0, c).start()

    def in_stage(d, u):
        b = u // NC

        if d == 0:

            @pl.when((u % NC == 0) & jnp.logical_not(keep[0]))
            def _():
                w_wait(0, b)

            @pl.when(u == 2)
            def _():
                pair_start(2)

            @pl.when((u == NC - 2) & keep[0])
            def _():
                w_wait(0, 1)
                pass_on(1)

        else:

            @pl.when(u == 0)
            def _():
                pair_wait(d)
                remote(w1.at[d], w1.at[d], s_w.at[d], r_w.at[d, 0], mate).wait_recv()

        if d == 0:

            @pl.when((u + AHEAD >= NC) & (u + AHEAD < NU))
            def _():
                in_copy(0, u + AHEAD).start()

            for part in range(8):

                @pl.when((u == PIECE_AT[part]) & jnp.logical_not(keep[0]))
                def _(part=part):
                    w_copy(0, 1, part, a_of[0]).start()

        in_copy(d, u).wait_recv()
        pair = jnp.concatenate([pn[d, u, half[d]], rsw[d, u]], axis=1)
        n = mm(pair, w1[d, b]).astype(BF)
        ya = mm(n[:, :R], w2[d, 0, b])
        yb = mm(n[:, R:], w2[d, 1, b])
        xs[d, u, 0] = ya[:, :R].astype(BF)
        xs[d, u, 1] = yb[:, :R].astype(BF)
        mid_copy(d, u).start()
        st[d, u % 4, 0] = ya[:, R:]
        st[d, u % 4, 1] = yb[:, R:]

    def mid_stage(d, u):
        mid_copy(d, u).wait_recv()
        bs[d, u] = (st[d, u % 4, 1] + xr[d, u, 0].astype(F32)).astype(BF)
        back_copy(d, u, True).start()
        pn[d + 1, u, half[d]] = (st[d, u % 4, 0] + xr[d, u, 1].astype(F32)).astype(BF)

    def back_stage(d, u):
        back_copy(d, u, False).wait_recv()
        if d < 2:
            in_copy(d + 1, u).start()
        else:
            fin_copy(u).start()

    def out_stage(d, u):
        b = u // NC
        c = u % NC

        some = rsw.at[0, pl.ds(0, NC // 2)]

        @pl.when((u % 4 == 0) & (b == 0) & (me > 0))
        def _():
            remote(some, some, s_halo.at[0], r_halo.at[0, c // 4], right).wait_recv()

        @pl.when((u % 4 == 0) & (b == 1) & (me < count - 1))
        def _():
            remote(some, some, s_halo.at[1], r_halo.at[1, c // 4], left).wait_recv()

        fin_copy(u).wait_recv()
        cols = pl.ds(pl.multiple_of(b * B, B), B + 2 * H)
        for at, proxy in ((core, pn[3, u, core]), (1 - core, fin[u])):
            rows = pl.ds(pl.multiple_of(at * HALF, HALF), HALF)
            both = jnp.concatenate([win[c, rows, cols], proxy], axis=1)
            obuf[u, rows, :] = mm(both, wo[b]).astype(BF)
        for h in range(2):
            out_copy(u, h).start()

    def begin(i):
        @pl.when(i < NC)
        def _():
            leaf_stage(i)

            @pl.when(i == PAIR_AT)
            def _():
                pair_start(0)

        @pl.when((i > 0) & (i <= NC))
        def _():
            one_stage(i - 1)

    def prologue(i, _):
        begin(i)
        return 0

    lax.fori_loop(0, BEFORE, prologue, 0)
    load_wait(3)
    pair_wait(0)

    @pl.when(keep[0])
    def _():
        w_wait(0, 0)
        pass_on(0)

    pair_start(1)

    bodies = {"in": in_stage, "mid": mid_stage, "back": back_stage}

    def step(t, _):
        begin(t + BEFORE)
        for kind, d in STAGES:
            a, b = t - LAG_A[kind][d], t - LAG_B[kind][d]
            u = jnp.where(a < FIRST, a, b)

            @pl.when((a >= 0) & ((a < FIRST) | (b >= FIRST)) & (u < NU))
            def _(u=u, kind=kind, d=d):
                bodies[kind](d, u)

        def outs(t):
            a, b = t + 1 - OUT_LAG - LAG_A["back"][2], t + 1 - OUT_LAG - LAG_B["back"][2]
            came = jnp.where(a < FIRST, a, jnp.maximum(b, FIRST))
            return jnp.clip(jnp.minimum(came, OUT_RATE * (t - OUT_AT + 1)), 0, NU)

        def result(u, _):
            out_stage(2, u)
            return 0

        lax.fori_loop(outs(t - 1), outs(t), result, 0)

        @pl.when((t >= HALO_AT) & (t < HALO_AT + 2))
        def _():
            for k in range(4):
                halo_send(4 * (t - HALO_AT) + k, 1)

        return 0

    lax.fori_loop(0, STEPS, step, 0)

    local(obuf, obuf, l_out).wait()
    remote(xr1, xr1, s_one, r_one.at[0, 0], mate).wait_send()
    for d in range(3):
        remote(rsw.at[d], rsw.at[d], s_in.at[d], r_in.at[d, 0], a_of[d]).wait_send()
        remote(xs.at[d], xr.at[d], s_mid.at[d], r_mid.at[d, 0], b_of[d]).wait_send()
        remote(bs.at[d], bs.at[d], s_back.at[d], r_back.at[d, 0], a_of[d]).wait_send()
        sent = w1.at[0] if d == 0 else w1.at[pl.ds(0, 2)]

        @pl.when(keep[d])
        def _(d=d):
            remote(w1.at[d], w1.at[d], s_pair.at[d], r_pair.at[d], mate).wait_send()

        @pl.when(jnp.logical_not(keep[d]))
        def _(d=d, sent=sent):
            remote(sent, sent, s_w.at[d], r_w.at[d, 0], a_of[d]).wait_send()

    @pl.when(keep[0])
    def _():
        remote(w1.at[0], w1.at[0], s_pass, r_w.at[0, 0], mate).wait_send()

    remote(wl.at[:, hi], wl.at[:, hi], s_level, r_level, mate).wait_send()
    remote(fin, fin, s_fin, r_fin.at[0], mate).wait_send()
    whole = rsw.at[0, pl.ds(0, NC)]

    @pl.when(me < count - 1)
    def _():
        remote(whole, whole, s_halo.at[0], r_halo.at[0, 0], right).wait_send()

    @pl.when(me > 0)
    def _():
        remote(whole, whole, s_halo.at[1], r_halo.at[1, 0], left).wait_send()


def widen_kernel(x_h, o_h, x_v, o_v, l_in, l_out):
    parts = NV // WROWS

    def get(i):
        return pltpu.make_async_copy(x_h.at[pl.ds(i * WROWS, WROWS)], x_v.at[i], l_in.at[i])

    def put(i):
        return pltpu.make_async_copy(o_v.at[i], o_h.at[pl.ds(i * WROWS, WROWS)], l_out.at[i])

    for i in range(parts):
        get(i).start()
    for i in range(parts):
        get(i).wait()
        o_v[i] = x_v[i].astype(F32)
        put(i).start()
    for i in range(parts):
        put(i).wait()


def widen(x):
    parts = NV // WROWS
    spec = pl.BlockSpec(memory_space=pl.ANY)
    return pl.pallas_call(
        widen_kernel, in_specs=[spec], out_specs=spec,
        out_shape=jax.ShapeDtypeStruct((NV, 2 * B), F32),
        scratch_shapes=[
            pltpu.VMEM((parts, WROWS, 2 * B), BF), pltpu.VMEM((parts, WROWS, 2 * B), F32),
            pltpu.SemaphoreType.DMA((parts,)), pltpu.SemaphoreType.DMA((parts,)),
        ],
        compiler_params=pltpu.CompilerParams(vmem_limit_bytes=60_000_000),
    )(x)


def per_device(sources, leaf_basis, stay_blocks, cross_blocks, out_basis, near_blocks):
    dma = pltpu.SemaphoreType.DMA
    v = pltpu.VMEM
    scratch = [
        v((SLOTS, CH, 2 * B), F32),
        v(leaf_basis.shape, BF),
        v((2 * R, 2 * R), BF),
        v((2, 2 * R, 2 * R), BF),
        v((3, 2, 2 * R, 2 * R), BF),
        v((3, 2, 2, R, 2 * R), BF),
        v((2, B + 2 * H + R, B), BF),
        v((NC, CH, 2 * B + 2 * H), BF),
        v((NU, 2, HALF, R), BF),
        v((NU, HALF, R), BF),
        v((4, NU, 2, HALF, R), BF),
        v((3, NU, HALF, R), BF),
        v((3, 4, 2, HALF, R), F32),
        v((3, NU, 2, HALF, R), BF),
        v((3, NU, 2, HALF, R), BF),
        v((3, NU, HALF, R), BF),
        v((NU, HALF, R), BF),
        v((NU, CH, B), BF),
        dma((SLOTS,)), dma((7,)), dma,
        dma((2, 4)), dma((3, KEYS)), dma((3, KEYS)), dma((3, KEYS)), dma((2, 2)), dma((3, 2)), dma((3,)), dma, dma((NU,)),
        dma, dma((3,)), dma((3,)), dma((3,)), dma((2,)), dma((3,)), dma((3,)), dma, dma, dma,
    ]
    out = pl.pallas_call(
        kernel,
        out_shape=jax.ShapeDtypeStruct((NV, 2 * B), BF),
        in_specs=[pl.BlockSpec(memory_space=pl.ANY)] * 6,
        out_specs=pl.BlockSpec(memory_space=pl.ANY),
        scratch_shapes=scratch,
        compiler_params=pltpu.CompilerParams(
            collective_id=0, has_side_effects=True, vmem_limit_bytes=66_900_000
        ),
    )(sources, leaf_basis, stay_blocks, cross_blocks, out_basis, near_blocks)
    return widen(out)


def solution(mesh):
    in_specs = (
        P(None, "box"),
        P("box", None, None),
        P(None, "box", None, None),
        P(None, "box", None, None),
        P("box", None, None),
        P("box", None, None),
    )
    return jax.shard_map(
        per_device, mesh=mesh, in_specs=in_specs, out_specs=P(None, "box"), check_vma=False
    )
```

```python
import jax
import jax.numpy as jnp
from jax import lax
from jax.experimental import pallas as pl
from jax.experimental.pallas import tpu as pltpu
from jax.sharding import PartitionSpec as P

MESH = pl.DeviceIdType.MESH
BF = jnp.bfloat16
F32 = jnp.float32

B = 512
H = 128
R = 256
NV = 2048
CH = 256
NC = NV // CH
NU = 2 * NC
HALF = CH // 2
SLOTS = 4

STRIDE = (2, 8, 32)
AHEAD = 2
BEFORE = AHEAD + 1
STAGES = (("back", 0), ("back", 1), ("back", 2), ("in", 0), ("mid", 0), ("in", 1), ("mid", 1), ("in", 2), ("mid", 2))
FIRST = 8
AT_A = (0, 2, 4, 5, 7, 9, 10, 12, 14)
AT_B = (0, 2, 4, 5, 7, 9, 10, 12, 14)
LAG_A = dict(zip(("in", "mid", "back"), (AT_A[0::3], AT_A[1::3], AT_A[2::3])))
LAG_B = dict(zip(("in", "mid", "back"), (AT_B[0::3], AT_B[1::3], AT_B[2::3])))
OUT_LAG = 1
STEPS = NU + LAG_B["back"][2] + OUT_LAG
HALO_AT = NU + 1
OUT_AT = HALO_AT + 2
OUT_RATE = 3
PAIR_AT = 0
PIECE_AT = (2, 2, 3, 3, 4, 4, 5, 5)
KEYS = 6
WROWS = 128


def mm(a, b):
    return jnp.dot(a, b, preferred_element_type=F32)


def kernel(
    src_h, leaf_h, stay_h, cross_h, outb_h, near_h, out_h,
    src_v, leaf_v, w0, wl, w1, w2, wo, win, n1, xr1, pn, rsw, st, xs, xr, bs, fin, obuf,
    l_src, l_w, l_out,
    r_one, r_in, r_mid, r_back, r_halo, r_w, r_pair, r_level, r_fin,
    s_one, s_in, s_mid, s_back, s_halo, s_w, s_pair, s_level, s_pass, s_fin,
):
    me = lax.axis_index("box")
    core = me % 2
    mate = me + 1 - 2 * core
    pos = [(me // st) % 4 for st in STRIDE]
    a_of = [me + (1 - 2 * (v % 2)) * st for v, st in zip(pos, STRIDE)]
    b_of = [me + (3 - 2 * v) * st for v, st in zip(pos, STRIDE)]
    half = [(v % 2 + v // 2) % 2 for v in pos]
    count = lax.axis_size("box")
    right = (me + 1) % count
    left = (me + count - 1) % count

    def local(src, dst, sem):
        return pltpu.make_async_copy(src, dst, sem)

    def remote(src, dst, ssem, rsem, to):
        return pltpu.make_async_remote_copy(
            src_ref=src, dst_ref=dst, send_sem=ssem, recv_sem=rsem,
            device_id=(to,), device_id_type=MESH,
        )

    def src_start(c):
        for h in range(2):
            rows = pl.ds(h * (NV // 2) + c * HALF, HALF)
            local(src_h.at[rows], src_v.at[c % SLOTS, pl.ds(h * HALF, HALF)], l_src.at[c % SLOTS]).start()

    def src_wait(c):
        local(src_v.at[c % SLOTS], src_v.at[c % SLOTS], l_src.at[c % SLOTS]).wait()

    keep = [core == h for h in half]
    lo, hi = pl.ds(0, R), pl.ds(R, R)
    loads = [[(leaf_h, leaf_v)]]
    loads += [[(stay_h.at[0, 0], w0.at[lo, lo]), (cross_h.at[0, 0], w0.at[lo, hi]),
               (cross_h.at[0, 1], w0.at[hi, lo]), (stay_h.at[0, 1], w0.at[hi, hi])]]
    loads += [[(stay_h.at[1], wl.at[:, lo, lo]), (cross_h.at[1], wl.at[:, lo, hi])]]
    loads += [[(near_h, wo.at[:, pl.ds(0, B + 2 * H)]), (outb_h, wo.at[:, pl.ds(B + 2 * H, R)])]]
    loaded = [leaf_v, w0, wl.at[:, lo], wo]

    def load(i):
        for src, dst in loads[i]:
            local(src, dst, l_w.at[i]).start()

    def load_wait(i):
        local(loaded[i], loaded[i], l_w.at[i]).wait()

    src_start(0)
    for i in range(3):
        load(i)

    barrier = pltpu.get_barrier_semaphore()
    other_of = [a + 1 - 2 * core for a in a_of]
    peers = [mate] + a_of + other_of[1:] + b_of + [left, right]
    for to in peers:
        pl.semaphore_signal(barrier, inc=1, device_id=(to,), device_id_type=MESH)
    pl.semaphore_wait(barrier, len(peers))

    def w_copy(d, b, part, to):
        some = pl.ds((part % 2) * (R // 2), R // 2)
        there = pl.ds(R + (part % 2) * (R // 2), R // 2)
        src, dst = (
            (stay_h.at[2 + 2 * d, b, some], w1.at[d, b, there, hi]),
            (cross_h.at[2 + 2 * d, b, some], w1.at[d, b, there, lo]),
            (cross_h.at[3 + 2 * d, b, some], w2.at[d, 1, b, some, lo]),
            (stay_h.at[3 + 2 * d, b, some], w2.at[d, 1, b, some, hi]),
        )[part // 2]
        return remote(src, dst, s_w.at[d], r_w.at[d, b], to)

    def pair_blocks(d):
        return (
            (stay_h.at[2 + 2 * d], w1.at[d, :, lo, lo]),
            (cross_h.at[2 + 2 * d], w1.at[d, :, lo, hi]),
            (cross_h.at[3 + 2 * d], w2.at[d, 0, :, :, lo]),
            (stay_h.at[3 + 2 * d], w2.at[d, 0, :, :, hi]),
        )

    def pass_on(b):
        for ref in (w1.at[0, b, hi], w2.at[0, 1, b]):
            remote(ref, ref, s_pass, r_w.at[0, b], mate).start()

    def w_wait(d, b):
        whole = w1.at[d, b]
        remote(whole, whole, s_w.at[d], r_w.at[d, b], mate).wait_recv()

    @pl.when(jnp.logical_not(keep[0]))
    def _():
        for part in range(8):
            w_copy(0, 0, part, a_of[0]).start()

    for src, dst in ((stay_h.at[1], wl.at[:, hi, hi]), (cross_h.at[1], wl.at[:, hi, lo])):
        remote(src, dst, s_level, r_level, mate).start()
    def pair_start(d):
        @pl.when(keep[d])
        def _():
            for src, dst in pair_blocks(d):
                local(src, dst, l_w.at[4 + d]).start()
                remote(src, dst, s_pair.at[d], r_pair.at[d], mate).start()

    def pair_wait(d):
        @pl.when(keep[d])
        def _():
            local(w1.at[d], w1.at[d], l_w.at[4 + d]).wait()

        @pl.when(jnp.logical_not(keep[d]))
        def _():
            remote(w1.at[d], w1.at[d], s_pair.at[d], r_pair.at[d], mate).wait_recv()

    for d in (1, 2):

        @pl.when(jnp.logical_not(keep[d]))
        def _(d=d):
            for to in (a_of[d], other_of[d]):
                for src, dst in (
                    (stay_h.at[2 + 2 * d], w1.at[d, :, hi, hi]),
                    (cross_h.at[2 + 2 * d], w1.at[d, :, hi, lo]),
                    (cross_h.at[3 + 2 * d], w2.at[d, 1, :, :, lo]),
                    (stay_h.at[3 + 2 * d], w2.at[d, 1, :, :, hi]),
                ):
                    remote(src, dst, s_w.at[d], r_w.at[d, 0], to).start()

    for c in range(1, SLOTS):
        src_start(c)
    load(3)

    @pl.when(me == 0)
    def _():
        for c in range(NC):
            win[c, :, 0:H] = jnp.zeros((CH, H), BF)

    @pl.when(me == count - 1)
    def _():
        for c in range(NC):
            win[c, :, H + 2 * B :] = jnp.zeros((CH, H), BF)

    for i in range(3):
        load_wait(i)
    remote(wl.at[:, hi], wl.at[:, hi], s_level, r_level, mate).wait_recv()

    def one_copy(u):
        return remote(n1.at[u, 1 - core], xr1.at[u], s_one, r_one.at[u // NC, u % 4], mate)

    def in_copy(d, u):
        return remote(pn.at[d, u, 1 - half[d]], rsw.at[d, u], s_in.at[d], r_in.at[d, u % KEYS], a_of[d])

    def mid_copy(d, u):
        return remote(xs.at[d, u], xr.at[d, u], s_mid.at[d], r_mid.at[d, u % KEYS], b_of[d])

    def back_copy(d, u, mine):
        at = half[d] if mine else 1 - half[d]
        return remote(bs.at[d, u], pn.at[d + 1, u, at], s_back.at[d], r_back.at[d, u % KEYS], a_of[d])

    def fin_copy(u):
        return remote(pn.at[3, u, 1 - core], fin.at[u], s_fin, r_fin.at[u], mate)

    def halo_copy(side, c):
        if side == 0:
            return remote(
                win.at[c, :, pl.ds(2 * B, H)], win.at[c, :, pl.ds(0, H)], s_halo.at[0], r_halo.at[0, c // 4], right
            )
        return remote(
            win.at[c, :, pl.ds(H, H)], win.at[c, :, pl.ds(H + 2 * B, H)], s_halo.at[1], r_halo.at[1, c // 4], left
        )

    late = ((core == 1) & (pos[0] % 2 == 0), (core == 0) & (pos[0] % 2 == 1))

    def halo_send(c, when):
        for side, there in ((0, me < count - 1), (1, me > 0)):
            chosen = late[side] if when else jnp.logical_not(late[side])

            @pl.when(there & chosen)
            def _(side=side):
                halo_copy(side, c).start()

    def out_copy(u, h):
        rows = pl.ds(h * (NV // 2) + (u % NC) * HALF, HALF)
        cols = pl.ds(pl.multiple_of((u // NC) * B, B), B)
        return local(obuf.at[u, pl.ds(h * HALF, HALF)], out_h.at[rows, cols], l_out)

    def leaf_stage(c):
        src_wait(c)
        for h in range(2):
            rows = pl.ds(h * HALF, HALF)
            cells = src_v[c % SLOTS, rows, :].astype(BF)
            win[c, rows, H : H + 2 * B] = cells
            p0 = mm(cells[:, :B], leaf_v[0]).astype(BF)
            p1 = mm(cells[:, B:], leaf_v[1]).astype(BF)
            n = mm(jnp.concatenate([p0, p1], axis=1), w0[...]).astype(BF)
            n1[c, h] = n[:, :R]
            n1[NC + c, h] = n[:, R:]
        one_copy(c).start()
        one_copy(NC + c).start()

        @pl.when(c + SLOTS < NC)
        def _():
            src_start(c + SLOTS)

    def one_stage(c):
        for b in range(2):
            u = b * NC + c
            one_copy(u).wait_recv()
            pair = jnp.concatenate([n1[u, core], xr1[u]], axis=1)
            p = mm(pair, wl[b]).astype(BF)
            pn[0, u, core] = p[:, :R]
            pn[0, u, 1 - core] = p[:, R:]

        halo_send(c, 0)

        in_copy(0, c).start()

    def in_stage(d, u):
        b = u // NC

        if d == 0:

            @pl.when((u % NC == 0) & jnp.logical_not(keep[0]))
            def _():
                w_wait(0, b)

            @pl.when(u == 2)
            def _():
                pair_start(2)

            @pl.when((u == NC - 2) & keep[0])
            def _():
                w_wait(0, 1)
                pass_on(1)

        else:

            @pl.when(u == 0)
            def _():
                pair_wait(d)
                remote(w1.at[d], w1.at[d], s_w.at[d], r_w.at[d, 0], mate).wait_recv()

        if d == 0:

            @pl.when((u + AHEAD >= NC) & (u + AHEAD < NU))
            def _():
                in_copy(0, u + AHEAD).start()

            for part in range(8):

                @pl.when((u == PIECE_AT[part]) & jnp.logical_not(keep[0]))
                def _(part=part):
                    w_copy(0, 1, part, a_of[0]).start()

        in_copy(d, u).wait_recv()
        pair = jnp.concatenate([pn[d, u, half[d]], rsw[d, u]], axis=1)
        n = mm(pair, w1[d, b]).astype(BF)
        ya = mm(n[:, :R], w2[d, 0, b])
        yb = mm(n[:, R:], w2[d, 1, b])
        xs[d, u, 0] = ya[:, :R].astype(BF)
        xs[d, u, 1] = yb[:, :R].astype(BF)
        mid_copy(d, u).start()
        st[d, u % 4, 0] = ya[:, R:]
        st[d, u % 4, 1] = yb[:, R:]

    def mid_stage(d, u):
        mid_copy(d, u).wait_recv()
        bs[d, u] = (st[d, u % 4, 1] + xr[d, u, 0].astype(F32)).astype(BF)
        back_copy(d, u, True).start()
        pn[d + 1, u, half[d]] = (st[d, u % 4, 0] + xr[d, u, 1].astype(F32)).astype(BF)

    def back_stage(d, u):
        back_copy(d, u, False).wait_recv()
        if d < 2:
            in_copy(d + 1, u).start()
        else:
            fin_copy(u).start()

    def out_stage(d, u):
        b = u // NC
        c = u % NC

        some = rsw.at[0, pl.ds(0, NC // 2)]

        @pl.when((u % 4 == 0) & (b == 0) & (me > 0))
        def _():
            remote(some, some, s_halo.at[0], r_halo.at[0, c // 4], right).wait_recv()

        @pl.when((u % 4 == 0) & (b == 1) & (me < count - 1))
        def _():
            remote(some, some, s_halo.at[1], r_halo.at[1, c // 4], left).wait_recv()

        fin_copy(u).wait_recv()
        cols = pl.ds(pl.multiple_of(b * B, B), B + 2 * H)
        for at, proxy in ((core, pn[3, u, core]), (1 - core, fin[u])):
            rows = pl.ds(pl.multiple_of(at * HALF, HALF), HALF)
            both = jnp.concatenate([win[c, rows, cols], proxy], axis=1)
            obuf[u, rows, :] = mm(both, wo[b]).astype(BF)
        for h in range(2):
            out_copy(u, h).start()

    def begin(i):
        @pl.when(i < NC)
        def _():
            leaf_stage(i)

            @pl.when(i == PAIR_AT)
            def _():
                pair_start(0)

        @pl.when((i > 0) & (i <= NC))
        def _():
            one_stage(i - 1)

    def prologue(i, _):
        begin(i)
        return 0

    lax.fori_loop(0, BEFORE, prologue, 0)
    load_wait(3)
    pair_wait(0)

    @pl.when(keep[0])
    def _():
        w_wait(0, 0)
        pass_on(0)

    pair_start(1)

    bodies = {"in": in_stage, "mid": mid_stage, "back": back_stage}

    def step(t, _):
        begin(t + BEFORE)
        for kind, d in STAGES:
            a, b = t - LAG_A[kind][d], t - LAG_B[kind][d]
            u = jnp.where(a < FIRST, a, b)

            @pl.when((a >= 0) & ((a < FIRST) | (b >= FIRST)) & (u < NU))
            def _(u=u, kind=kind, d=d):
                bodies[kind](d, u)

        def outs(t):
            a, b = t + 1 - OUT_LAG - LAG_A["back"][2], t + 1 - OUT_LAG - LAG_B["back"][2]
            came = jnp.where(a < FIRST, a, jnp.maximum(b, FIRST))
            return jnp.clip(jnp.minimum(came, OUT_RATE * (t - OUT_AT + 1)), 0, NU)

        def result(u, _):
            out_stage(2, u)
            return 0

        lax.fori_loop(outs(t - 1), outs(t), result, 0)

        @pl.when((t >= HALO_AT) & (t < HALO_AT + 2))
        def _():
            for k in range(4):
                halo_send(4 * (t - HALO_AT) + k, 1)

        return 0

    lax.fori_loop(0, STEPS, step, 0)

    local(obuf, obuf, l_out).wait()
    remote(xr1, xr1, s_one, r_one.at[0, 0], mate).wait_send()
    for d in range(3):
        remote(rsw.at[d], rsw.at[d], s_in.at[d], r_in.at[d, 0], a_of[d]).wait_send()
        remote(xs.at[d], xr.at[d], s_mid.at[d], r_mid.at[d, 0], b_of[d]).wait_send()
        remote(bs.at[d], bs.at[d], s_back.at[d], r_back.at[d, 0], a_of[d]).wait_send()
        sent = w1.at[0] if d == 0 else w1.at[pl.ds(0, 2)]

        @pl.when(keep[d])
        def _(d=d):
            remote(w1.at[d], w1.at[d], s_pair.at[d], r_pair.at[d], mate).wait_send()

        @pl.when(jnp.logical_not(keep[d]))
        def _(d=d, sent=sent):
            remote(sent, sent, s_w.at[d], r_w.at[d, 0], a_of[d]).wait_send()

    @pl.when(keep[0])
    def _():
        remote(w1.at[0], w1.at[0], s_pass, r_w.at[0, 0], mate).wait_send()

    remote(wl.at[:, hi], wl.at[:, hi], s_level, r_level, mate).wait_send()
    remote(fin, fin, s_fin, r_fin.at[0], mate).wait_send()
    whole = rsw.at[0, pl.ds(0, NC)]

    @pl.when(me < count - 1)
    def _():
        remote(whole, whole, s_halo.at[0], r_halo.at[0, 0], right).wait_send()

    @pl.when(me > 0)
    def _():
        remote(whole, whole, s_halo.at[1], r_halo.at[1, 0], left).wait_send()


def widen_kernel(x_h, o_h, x_v, o_v, l_in, l_out):
    parts = NV // WROWS

    def get(i):
        return pltpu.make_async_copy(x_h.at[pl.ds(i * WROWS, WROWS)], x_v.at[i], l_in.at[i])

    def put(i):
        return pltpu.make_async_copy(o_v.at[i], o_h.at[pl.ds(i * WROWS, WROWS)], l_out.at[i])

    for i in range(parts):
        get(i).start()
    for i in range(parts):
        get(i).wait()
        o_v[i] = x_v[i].astype(F32)
        put(i).start()
    for i in range(parts):
        put(i).wait()


def widen(x):
    parts = NV // WROWS
    spec = pl.BlockSpec(memory_space=pl.ANY)
    return pl.pallas_call(
        widen_kernel, in_specs=[spec], out_specs=spec,
        out_shape=jax.ShapeDtypeStruct((NV, 2 * B), F32),
        scratch_shapes=[
            pltpu.VMEM((parts, WROWS, 2 * B), BF), pltpu.VMEM((parts, WROWS, 2 * B), F32),
            pltpu.SemaphoreType.DMA((parts,)), pltpu.SemaphoreType.DMA((parts,)),
        ],
        compiler_params=pltpu.CompilerParams(vmem_limit_bytes=60_000_000),
    )(x)


def per_device(sources, leaf_basis, stay_blocks, cross_blocks, out_basis, near_blocks):
    dma = pltpu.SemaphoreType.DMA
    v = pltpu.VMEM
    scratch = [
        v((SLOTS, CH, 2 * B), F32),
        v(leaf_basis.shape, BF),
        v((2 * R, 2 * R), BF),
        v((2, 2 * R, 2 * R), BF),
        v((3, 2, 2 * R, 2 * R), BF),
        v((3, 2, 2, R, 2 * R), BF),
        v((2, B + 2 * H + R, B), BF),
        v((NC, CH, 2 * B + 2 * H), BF),
        v((NU, 2, HALF, R), BF),
        v((NU, HALF, R), BF),
        v((4, NU, 2, HALF, R), BF),
        v((3, NU, HALF, R), BF),
        v((3, 4, 2, HALF, R), F32),
        v((3, NU, 2, HALF, R), BF),
        v((3, NU, 2, HALF, R), BF),
        v((3, NU, HALF, R), BF),
        v((NU, HALF, R), BF),
        v((NU, CH, B), BF),
        dma((SLOTS,)), dma((7,)), dma,
        dma((2, 4)), dma((3, KEYS)), dma((3, KEYS)), dma((3, KEYS)), dma((2, 2)), dma((3, 2)), dma((3,)), dma, dma((NU,)),
        dma, dma((3,)), dma((3,)), dma((3,)), dma((2,)), dma((3,)), dma((3,)), dma, dma, dma,
    ]
    out = pl.pallas_call(
        kernel,
        out_shape=jax.ShapeDtypeStruct((NV, 2 * B), BF),
        in_specs=[pl.BlockSpec(memory_space=pl.ANY)] * 6,
        out_specs=pl.BlockSpec(memory_space=pl.ANY),
        scratch_shapes=scratch,
        compiler_params=pltpu.CompilerParams(
            collective_id=0, has_side_effects=True, vmem_limit_bytes=66_900_000
        ),
    )(sources, leaf_basis, stay_blocks, cross_blocks, out_basis, near_blocks)
    return widen(out)


def solution(mesh):
    in_specs = (
        P(None, "box"),
        P("box", None, None),
        P(None, "box", None, None),
        P(None, "box", None, None),
        P("box", None, None),
        P("box", None, None),
    )
    return jax.shard_map(
        per_device, mesh=mesh, in_specs=in_specs, out_specs=P(None, "box"), check_vma=False
    )
```
